32 devices in a mesh: wide: 8 (over z, x), narrow: 4 (over y, core).
Axes of the slice: x: 2, y: 2, z: 4, core: 2. Of those that a mesh axis runs over, the one named last changes fastest.
Arguments:
- table: float32 [256, 256, 64, 128], P(None, 'narrow', 'wide'), may hold values from -200 to 200, as said below
- prior_one: float32 [256, 32], replicated, may hold values from -0.375 to 0.375
- factor_two: float32 [256, 32], replicated, may hold values from -0.375 to 0.375
- factor_three: float32 [64, 32], replicated, may hold values from -0.75 to 0.75
Outputs:
- core: float32 [32, 32, 32, 128], P('narrow', 'wide')
- basis: float32 [256, 32], replicated
The draws below stay inside these ranges and needn't reach their ends.
Inputs may be any that keep to these rules, and one draw needn't show every extreme that they name: Entries of the table lie within the stated bounds.
All inputs are finite; a program needn't handle non-finite values.
Results may differ from the reference program's by a relative error of at most 0.0003.
Values sent between devices are 32-bit elements; how exact they have to be, the bound alone decides.
A program may use at most 256 MiB of HBM per device.

```python
import jax
import jax.numpy as jnp
from jax import lax

I1 = 256
I2 = 256
I3 = 64
M = 128
R = 32
R2 = 32
R3 = 32
SUB = 2


def draw_table(key, part):
    keys = jax.random.split(key, 4)
    rows = jnp.exp(jax.random.uniform(keys[0], (I1, 1, 1, 1), jnp.float32, 0.0, 2.3))
    noise = jax.random.truncated_normal(keys[3], -5.0, 5.0, (I1, I2, I3, M), jnp.float32)
    second = jax.random.uniform(keys[1], (1, I2, 1, 1), jnp.float32, 0.5, 2.0)
    third = jax.random.uniform(keys[2], (1, 1, I3, 1), jnp.float32, 0.5, 2.0)
    return rows * second * third * noise


def bell_draw(own_key, shape, spread, limit, kind=jnp.bfloat16):
    result = spread * jax.random.normal(own_key, shape, jnp.float32)
    return jnp.clip(result, min=-limit, max=limit).astype(kind)


def setup_inputs(seed: int = 0) -> dict:
    streams_of = jax.random.split(jax.random.key(seed), 5)
    table = draw_table(jax.random.fold_in(streams_of[4], 71), 0)
    prior_one = bell_draw(streams_of[1], (I1, R), I1 ** -0.5, 0.375, jnp.float32)
    factor_two = bell_draw(streams_of[2], (I2, R2), I2 ** -0.5, 0.375, jnp.float32)
    factor_three = bell_draw(streams_of[3], (I3, R3), I3 ** -0.5, 0.75, jnp.float32)
    return {"table": table, "prior_one": prior_one, "factor_two": factor_two, "factor_three": factor_three}


HIGH = lax.Precision.HIGHEST

def orthonormal(q):
    s = jnp.dot(q.T.astype(jnp.float32), q.astype(jnp.float32), precision=HIGH, preferred_element_type=jnp.float32)
    lower = jnp.linalg.cholesky(s)
    return lax.linalg.triangular_solve(lower, q, left_side=False, lower=True, transpose_a=True)

def reference(table, prior_one, factor_two, factor_three):
    flat = table.reshape(I1, I2 * I3 * M)
    gram = jnp.dot(flat.astype(jnp.float32), flat.T.astype(jnp.float32), precision=HIGH, preferred_element_type=jnp.float32) / float(I2 * I3 * M)
    basis = prior_one
    for step in range(SUB):
        basis = orthonormal(jnp.dot(gram.astype(jnp.float32), basis.astype(jnp.float32), precision=HIGH, preferred_element_type=jnp.float32))
    cut_off = jnp.dot(basis.T.astype(jnp.float32), flat.astype(jnp.float32), precision=HIGH, preferred_element_type=jnp.float32).reshape(R, I2, I3, M)
    second = jnp.einsum('aijm,ib->abjm', cut_off, factor_two, precision=HIGH)
    core = jnp.einsum('abjm,jc->abcm', second, factor_three, precision=HIGH)
    return (core, basis)
```

```python
import functools

import jax
import jax.numpy as jnp
from jax import lax
from jax.experimental import pallas as pl
from jax.experimental.pallas import tpu as pltpu
from jax.sharding import PartitionSpec as P

I2 = 256
I3 = 64
M = 128
SUB = 2

F32 = jnp.float32
BF16 = jnp.bfloat16
HIGH = lax.Precision.HIGHEST
NT = (((1,), (1,)), ((), ()))
TN = (((0,), (0,)), ((), ()))


def split(x):
    hi = x.astype(BF16)
    return hi, (x - hi.astype(F32)).astype(BF16)


def gather_rows(ref, first, count, stride, lanes_of):
    flat = ref.reshape(count * stride, ref.shape[-1])
    parts = [flat[pl.ds(first + t, count, stride=stride), :] for t in range(lanes_of)]
    return jnp.concatenate(parts, axis=1)


def gram_kernel(group, table_ref, gram_ref, acc, cross):
    order, rows, _ = table_ref.shape
    step = pl.program_id(0)

    @pl.when(step == 0)
    def _():
        acc[...] = jnp.zeros_like(acc)
        cross[...] = jnp.zeros_like(cross)

    def body(g, carry):
        hi, lo = split(gather_rows(table_ref, g * group, order, rows, group))
        acc[...] += lax.dot_general(hi, hi, NT, preferred_element_type=F32)
        cross[...] += lax.dot_general(hi, lo, NT, preferred_element_type=F32)
        return carry

    lax.fori_loop(0, rows // group, body, 0)

    @pl.when(step == pl.num_programs(0) - 1)
    def _():
        gram_ref[...] = acc[...] + (cross[...] + cross[...].T)


def gram_of(flat):
    order, rows, cells = flat.shape
    block = min(32, rows)
    return pl.pallas_call(
        functools.partial(gram_kernel, min(8, block)),
        grid=(rows // block,),
        in_specs=[pl.BlockSpec((order, block, cells), lambda i: (0, i, 0))],
        out_specs=pl.BlockSpec((order, order), lambda i: (0, 0)),
        out_shape=jax.ShapeDtypeStruct((order, order), F32),
        scratch_shapes=[pltpu.VMEM((order, order), F32)] * 2,
        compiler_params=pltpu.CompilerParams(vmem_limit_bytes=48 << 20),
    )(flat)


def basis_kernel(scale, gram_ref, prior_ref, basis_ref, turned_ref):
    gram = gram_ref[...] * scale
    basis = prior_ref[...]
    rank = basis.shape[1]
    row = lax.broadcasted_iota(jnp.int32, (rank, 1), 0)
    lane = lax.broadcasted_iota(jnp.int32, (rank, rank), 1)
    square_row = lax.broadcasted_iota(jnp.int32, (rank, rank), 0)
    for _ in range(SUB):
        q = jnp.dot(gram, basis, precision=HIGH, preferred_element_type=F32)
        s = lax.dot_general(q, q, TN, precision=HIGH, preferred_element_type=F32)
        inverse = jnp.where(lane == square_row, 1.0, 0.0)
        root = jnp.ones((rank, 1), F32)
        for k in range(rank):
            pivot = s[k : k + 1, k : k + 1]
            root = jnp.where(row == k, lax.rsqrt(pivot), root)
            factor = jnp.where(row > k, s[:, k : k + 1] / pivot, 0.0)
            inverse = inverse - factor * inverse[k : k + 1, :]
            s = s - factor * s[k : k + 1, :]
        inverse = inverse * root
        basis = lax.dot_general(q, inverse, NT, precision=HIGH, preferred_element_type=F32)
    basis_ref[...] = basis
    turned_ref[...] = basis.T


def basis_of(gram, prior):
    scale = 1.0 / float(I2 * I3 * M)
    order, rank = prior.shape
    return pl.pallas_call(
        functools.partial(basis_kernel, scale),
        out_shape=(
            jax.ShapeDtypeStruct((order, rank), F32),
            jax.ShapeDtypeStruct((rank, order), F32),
        ),
    )(gram, prior)


def project_kernel(group, depth, turned_ref, two_ref, table_ref, out_ref, trunc):
    order, rows, cells = table_ref.shape
    rank = turned_ref.shape[0]
    total = trunc.shape[0] // rank
    tall = total // depth
    step = pl.program_id(0)
    left_hi, left_lo = split(turned_ref[...])
    left = jnp.concatenate([left_hi, left_lo], axis=0)

    def body(g, carry):
        hi, lo = split(gather_rows(table_ref, g * group, order, rows, group))
        both = jnp.dot(left, hi, preferred_element_type=F32)
        value = both[:rank] + (both[rank:] + jnp.dot(left_hi, lo, preferred_element_type=F32))
        for t in range(group):
            place = step * rows + g * group + t
            place = lax.rem(place, depth) * tall + place // depth
            trunc[pl.ds(place, rank, stride=total), :] = value[:, t * cells : (t + 1) * cells]
        return carry

    lax.fori_loop(0, rows // group, body, 0)

    @pl.when(step == pl.num_programs(0) - 1)
    def _():
        two_hi, two_lo = split(two_ref[...])
        two = jnp.concatenate([two_hi, two_lo], axis=0)
        width = two_ref.shape[0]

        def second(r, carry):
            parts = [
                trunc[pl.ds(pl.multiple_of(r * total + j * tall, tall), tall), :]
                for j in range(depth)
            ]
            hi, lo = split(jnp.concatenate(parts, axis=1))
            both = jnp.dot(two, hi, preferred_element_type=F32)
            value = both[:width] + (both[width:] + jnp.dot(two_hi, lo, preferred_element_type=F32))
            for j in range(depth):
                out_ref[pl.ds(r * width * depth + j, width, stride=depth), :] = value[
                    :, j * cells : (j + 1) * cells
                ]
            return carry

        lax.fori_loop(0, rank, second, 0)


def project(turned, two, flat, depth):
    order, rows, cells = flat.shape
    rank, width = turned.shape[0], two.shape[0]
    block = min(32, rows)
    return pl.pallas_call(
        functools.partial(project_kernel, min(8, block), depth),
        grid=(rows // block,),
        in_specs=[
            pl.BlockSpec(turned.shape, lambda i: (0, 0)),
            pl.BlockSpec(two.shape, lambda i: (0, 0)),
            pl.BlockSpec((order, block, cells), lambda i: (0, i, 0)),
        ],
        out_specs=pl.BlockSpec((rank * width * depth, cells), lambda i: (0, 0)),
        out_shape=jax.ShapeDtypeStruct((rank * width * depth, cells), F32),
        scratch_shapes=[pltpu.VMEM((rank * rows, cells), F32)],
        compiler_params=pltpu.CompilerParams(vmem_limit_bytes=56 << 20),
    )(turned, two, flat)


def per_device(narrow, wide, table, prior_one, factor_two, factor_three):
    order, rows_two, rows_three, cells = table.shape
    rank = prior_one.shape[1]
    width = factor_two.shape[1]
    flat = table.reshape(order, rows_two * rows_three, cells)
    gram = lax.psum(gram_of(flat), ("wide", "narrow"))
    basis, turned = basis_of(gram, prior_one)
    at = lax.axis_index("narrow")
    two = lax.dynamic_slice_in_dim(factor_two, at * rows_two, rows_two, 0).T
    part = project(turned, two, flat, rows_three)
    chips = narrow // 2
    core = at % 2
    part = part.reshape(chips, 2, rank // narrow, width, rows_three, cells)
    keep = lax.dynamic_index_in_dim(part, core, 1, keepdims=False)
    give = lax.dynamic_index_in_dim(part, 1 - core, 1, keepdims=False)
    swap = [(i, i ^ 1) for i in range(narrow)]
    part = keep + lax.ppermute(give, "narrow", swap)
    chip = at // 2
    mine = lax.dynamic_index_in_dim(part, chip, 0, keepdims=False)
    for hop in range(1, chips):
        perm = [(i, (i + 2 * hop) % narrow) for i in range(narrow)]
        there = lax.dynamic_index_in_dim(part, (chip + hop) % chips, 0, keepdims=False)
        mine = mine + lax.ppermute(there, "narrow", perm)
    mine = mine.reshape(rank // narrow, wide, width // wide, rows_three, cells)
    spread = lax.all_to_all(mine, "wide", split_axis=1, concat_axis=1, tiled=True)
    three = factor_three.reshape(wide, rows_three, factor_three.shape[1])
    core_out = jnp.einsum("rwbjm,wjc->rbcm", spread, three, precision=HIGH)
    return core_out, basis


def solution(mesh):
    return jax.shard_map(
        functools.partial(per_device, mesh.shape["narrow"], mesh.shape["wide"]),
        mesh=mesh,
        in_specs=(P(None, "narrow", "wide", None), P(), P(), P()),
        out_specs=(P("narrow", "wide", None, None), P()),
        check_vma=False,
    )
```

```python
import functools

import jax
import jax.numpy as jnp
from jax import lax
from jax.experimental import pallas as pl
from jax.experimental.pallas import tpu as pltpu
from jax.sharding import PartitionSpec as P

I2 = 256
I3 = 64
M = 128
SUB = 2

F32 = jnp.float32
BF16 = jnp.bfloat16
HIGH = lax.Precision.HIGHEST
NT = (((1,), (1,)), ((), ()))
TN = (((0,), (0,)), ((), ()))
MESH = pl.DeviceIdType.MESH


def split(x):
    hi = x.astype(BF16)
    return hi, (x - hi.astype(F32)).astype(BF16)


def gather_rows(ref, first, group):
    block = jnp.swapaxes(ref[:, pl.ds(pl.multiple_of(first, group), group), :], 0, 1)
    return jnp.concatenate([block[t] for t in range(group)], axis=1)


def gram_kernel(group, table_ref, gram_ref, acc, cross):
    rows = table_ref.shape[1]
    step = pl.program_id(0)

    @pl.when(step == 0)
    def _():
        acc[...] = jnp.zeros_like(acc)
        cross[...] = jnp.zeros_like(cross)

    def body(g, carry):
        hi, lo = split(gather_rows(table_ref, g * group, group))
        acc[...] += lax.dot_general(hi, hi, NT, preferred_element_type=F32)
        cross[...] += lax.dot_general(hi, lo, NT, preferred_element_type=F32)
        return carry

    lax.fori_loop(0, rows // group, body, 0)

    @pl.when(step == pl.num_programs(0) - 1)
    def _():
        gram_ref[...] = acc[...] + (cross[...] + cross[...].T)


def gram_of(flat):
    order, rows, cells = flat.shape
    block = min(32, rows)
    return pl.pallas_call(
        functools.partial(gram_kernel, min(16, block)),
        grid=(rows // block,),
        in_specs=[pl.BlockSpec((order, block, cells), lambda i: (0, i, 0))],
        out_specs=pl.BlockSpec((order, order), lambda i: (0, 0)),
        out_shape=jax.ShapeDtypeStruct((order, order), F32),
        scratch_shapes=[pltpu.VMEM((order, order), F32)] * 2,
        compiler_params=pltpu.CompilerParams(vmem_limit_bytes=48 << 20),
    )(flat)


def greet(narrow, wide, at, place):
    barrier = pltpu.get_barrier_semaphore()
    for d in range(1, narrow):
        pl.semaphore_signal(
            barrier, inc=1, device_id={"narrow": lax.rem(at + d, narrow)}, device_id_type=MESH
        )
    for d in range(1, wide):
        pl.semaphore_signal(
            barrier, inc=1, device_id={"wide": lax.rem(place + d, wide)}, device_id_type=MESH
        )


def send(src, dst, send_sem, recv_sem, axis, to):
    copy = pltpu.make_async_remote_copy(
        src_ref=src,
        dst_ref=dst,
        send_sem=send_sem,
        recv_sem=recv_sem,
        device_id={axis: to},
        device_id_type=MESH,
    )
    copy.start()
    return copy


def finish(copies):
    for copy in copies:
        copy.wait()


def basis_kernel(
    narrow, wide, scale, part_ref, prior_ref, basis_ref, turned_ref,
    box_n, mine, box_w, full, square, sn, rn, sw, rw, tw, vw, tn, vn,
):
    at, place = lax.axis_index("narrow"), lax.axis_index("wide")
    greet(narrow, wide, at, place)
    pl.semaphore_wait(pltpu.get_barrier_semaphore(), narrow + wide - 2)
    copies = []
    for d in range(1, narrow):
        to = lax.rem(at + d, narrow)
        copies.append(send(part_ref.at[to], box_n.at[d], sn.at[d], rn.at[d], "narrow", to))
    finish(copies)
    value = part_ref[at]
    for d in range(1, narrow):
        value = value + box_n[d]
    mine[...] = value
    copies = []
    for d in range(1, wide):
        to = lax.rem(place + d, wide)
        copies.append(send(mine.at[to], box_w.at[d], sw.at[d], rw.at[d], "wide", to))
    finish(copies)
    value = mine[place]
    for d in range(1, wide):
        value = value + box_w[d]
    full[at, place] = value * scale
    copies = []
    for d in range(1, wide):
        to = lax.rem(place + d, wide)
        own = full.at[at, place]
        copies.append(send(own, own, tw.at[d], vw.at[d], "wide", to))
    finish(copies)
    copies = []
    for d in range(1, narrow):
        to = lax.rem(at + d, narrow)
        own = full.at[at]
        copies.append(send(own, own, tn.at[d], vn.at[d], "narrow", to))
    finish(copies)
    small = full.shape[2]
    for i in range(narrow * wide):
        square[i * small : (i + 1) * small, :] = full[i // wide, i % wide]
    gram = square[...]
    basis = prior_ref[...]
    rank = basis.shape[1]
    row = lax.broadcasted_iota(jnp.int32, (rank, 1), 0)
    lane = lax.broadcasted_iota(jnp.int32, (rank, rank), 1)
    square_row = lax.broadcasted_iota(jnp.int32, (rank, rank), 0)
    for _ in range(SUB):
        q = jnp.dot(gram, basis, precision=HIGH, preferred_element_type=F32)
        s = lax.dot_general(q, q, TN, precision=HIGH, preferred_element_type=F32)
        inverse = jnp.where(lane == square_row, 1.0, 0.0)
        root = jnp.ones((rank, 1), F32)
        for k in range(rank):
            pivot = s[k : k + 1, k : k + 1]
            root = jnp.where(row == k, lax.rsqrt(pivot), root)
            factor = jnp.where(row > k, s[:, k : k + 1] / pivot, 0.0)
            inverse = inverse - factor * inverse[k : k + 1, :]
            s = s - factor * s[k : k + 1, :]
        inverse = inverse * root
        basis = lax.dot_general(q, inverse, NT, precision=HIGH, preferred_element_type=F32)
    basis_ref[...] = basis
    turned_ref[...] = basis.T


def basis_of(narrow, wide, gram, prior):
    scale = 1.0 / float(I2 * I3 * M)
    order, rank = prior.shape
    small = order // (narrow * wide)
    dma = pltpu.SemaphoreType.DMA
    return pl.pallas_call(
        functools.partial(basis_kernel, narrow, wide, scale),
        in_specs=[pl.BlockSpec(memory_space=pltpu.VMEM)] * 2,
        out_specs=[pl.BlockSpec(memory_space=pltpu.VMEM)] * 2,
        out_shape=(
            jax.ShapeDtypeStruct((order, rank), F32),
            jax.ShapeDtypeStruct((rank, order), F32),
        ),
        scratch_shapes=[
            pltpu.VMEM((narrow, wide, small, order), F32),
            pltpu.VMEM((wide, small, order), F32),
            pltpu.VMEM((wide, small, order), F32),
            pltpu.VMEM((narrow, wide, small, order), F32),
            pltpu.VMEM((order, order), F32),
            dma((narrow,)), dma((narrow,)),
            dma((wide,)), dma((wide,)),
            dma((wide,)), dma((wide,)),
            dma((narrow,)), dma((narrow,)),
        ],
        compiler_params=pltpu.CompilerParams(collective_id=1, has_side_effects=True),
    )(gram.reshape(narrow, wide, small, order), prior)


def project_kernel(
    group, depth, narrow, wide, spread, turned_ref, two_ref, table_ref, out_ref,
    trunc, second, core_box, chip_box, wide_box, sc, rc, sy, ry, sw, rw,
):
    _, rows, cells = table_ref.shape
    rank = turned_ref.shape[0]
    total = trunc.shape[0] // rank
    tall = total // depth
    step = pl.program_id(0)
    at, place = lax.axis_index("narrow"), lax.axis_index("wide")

    @pl.when(step == 0)
    def _():
        greet(narrow, wide, at, place)

    left_hi, left_lo = split(turned_ref[...])
    left = jnp.concatenate([left_hi, left_lo], axis=0)

    def body(g, carry):
        hi, lo = split(gather_rows(table_ref, g * group, group))
        both = jnp.dot(left, hi, preferred_element_type=F32)
        value = both[:rank] + (both[rank:] + jnp.dot(left_hi, lo, preferred_element_type=F32))
        for t in range(group):
            spot = step * rows + g * group + t
            spot = lax.rem(spot, depth) * tall + spot // depth
            trunc[pl.ds(spot, rank, stride=total), :] = value[:, t * cells : (t + 1) * cells]
        return carry

    lax.fori_loop(0, rows // group, body, 0)

    @pl.when(step == pl.num_programs(0) - 1)
    def _():
        pl.semaphore_wait(pltpu.get_barrier_semaphore(), narrow + wide - 2)
        two_hi, two_lo = split(two_ref[...])
        two = jnp.concatenate([two_hi, two_lo], axis=0)
        width = two_ref.shape[0]
        per = rank // narrow
        slab = width * depth
        chips = narrow // 2
        chip, core = at // 2, lax.rem(at, 2)
        chunk = 2 if per % 2 == 0 else 1
        chunks = per // chunk
        flat = second.reshape(rank * slab, cells)

        def compute(block, q):
            def one(k, carry):
                r = block * per + q * chunk + k
                parts = [
                    trunc[pl.ds(pl.multiple_of(r * total + j * tall, tall), tall), :]
                    for j in range(depth)
                ]
                hi, lo = split(jnp.concatenate(parts, axis=1))
                both = jnp.dot(two, hi, preferred_element_type=F32)
                value = both[:width] + (
                    both[width:] + jnp.dot(two_hi, lo, preferred_element_type=F32)
                )
                for j in range(depth):
                    flat[pl.ds(r * slab + j, width, stride=depth), :] = value[
                        :, j * cells : (j + 1) * cells
                    ]
                return carry

            lax.fori_loop(0, chunk, one, 0)

        def part(q):
            return pl.ds(q * chunk, chunk)

        def target(h):
            return lax.rem(chip + h, chips)

        to_core, to_chip, to_wide = {}, {}, []

        def start(h, q):
            other = target(h) * 2 + (1 - core)
            compute(other, q)
            to_core[h, q] = send(
                second.at[other, part(q)], core_box.at[h, part(q)],
                sc.at[h, q], rc.at[h, q], "narrow", chip * 2 + (1 - core),
            )
            compute(target(h) * 2 + core, q)

        def merge(h, q):
            to_core[h, q].wait_recv()
            block = target(h) * 2 + core
            second[block, part(q)] = second[block, part(q)] + core_box[h, part(q)]
            if h:
                to_chip[h, q] = send(
                    second.at[block, part(q)], chip_box.at[h - 1, part(q)],
                    sy.at[h, q], ry.at[h, q], "narrow", block,
                )

        pairs = [(h, q) for h in [*range(1, chips), 0] for q in range(chunks)]
        for i, pair in enumerate(pairs):
            start(*pair)
            if i:
                merge(*pairs[i - 1])
        merge(*pairs[-1])
        for q in range(chunks):
            value = second[at, part(q)]
            for h in range(1, chips):
                to_chip[h, q].wait_recv()
                value = value + chip_box[h - 1, part(q)]
            if not spread:
                out_ref[0, part(q)] = value
                continue
            second[at, part(q)] = value
            band = slab // wide
            for d in range(1, wide):
                to = lax.rem(place + d, wide)
                rows_to = pl.ds(pl.multiple_of(to * band, band), band)
                to_wide.append(
                    send(
                        second.at[at, part(q), rows_to], wide_box.at[place, part(q)],
                        sw.at[d, q], rw.at[d, q], "wide", to,
                    )
                )
            own = pl.ds(pl.multiple_of(place * band, band), band)
            out_ref[place, part(q)] = second[at, part(q), own]
        for copy in [*to_core.values(), *to_chip.values()]:
            copy.wait_send()
        finish(to_wide)
        if spread:
            for d in range(1, wide):
                source = lax.rem(place + d, wide)
                out_ref[source] = wide_box[source]


def project(narrow, wide, turned, two, flat, depth):
    order, rows, cells = flat.shape
    rank, width = turned.shape[0], two.shape[0]
    block = min(32, rows)
    per, slab, chips = rank // narrow, width * depth, narrow // 2
    spread = (slab // wide) % 8 == 0
    shape = (wide, per, slab // wide, cells) if spread else (1, per, slab, cells)
    chunks = per // 2 if per % 2 == 0 else per
    dma = pltpu.SemaphoreType.DMA
    out = pl.pallas_call(
        functools.partial(
            project_kernel, min(16, block), depth, narrow, wide, spread
        ),
        grid=(rows // block,),
        in_specs=[
            pl.BlockSpec(turned.shape, lambda i: (0, 0)),
            pl.BlockSpec(two.shape, lambda i: (0, 0)),
            pl.BlockSpec((order, block, cells), lambda i: (0, i, 0)),
        ],
        out_specs=pl.BlockSpec(shape, lambda i: (0, 0, 0, 0)),
        out_shape=jax.ShapeDtypeStruct(shape, F32),
        scratch_shapes=[
            pltpu.VMEM((rank * rows, cells), F32),
            pltpu.VMEM((narrow, per, slab, cells), F32),
            pltpu.VMEM((chips, per, slab, cells), F32),
            pltpu.VMEM((max(chips - 1, 1), per, slab, cells), F32),
            pltpu.VMEM(shape, F32),
            dma((chips, chunks)), dma((chips, chunks)),
            dma((chips, chunks)), dma((chips, chunks)),
            dma((wide, chunks)), dma((wide, chunks)),
        ],
        compiler_params=pltpu.CompilerParams(
            vmem_limit_bytes=56 << 20, collective_id=2, has_side_effects=True
        ),
    )(turned, two, flat)
    if not spread:
        out = out.reshape(per, wide, slab // wide, cells)
        out = lax.all_to_all(out, "wide", split_axis=1, concat_axis=1, tiled=True)
        out = out.transpose(1, 0, 2, 3)
    return out.reshape(wide, per, width // wide, depth, cells)


def per_device(narrow, wide, table, prior_one, factor_two, factor_three):
    order, rows_two, rows_three, cells = table.shape
    flat = table.reshape(order, rows_two * rows_three, cells)
    basis, turned = basis_of(narrow, wide, gram_of(flat), prior_one)
    at = lax.axis_index("narrow")
    two = lax.dynamic_slice_in_dim(factor_two, at * rows_two, rows_two, 0).T
    spread = project(narrow, wide, turned, two, flat, rows_three)
    three = factor_three.reshape(wide, rows_three, factor_three.shape[1])
    core_out = jnp.einsum("wrbjm,wjc->rbcm", spread, three, precision=HIGH)
    return core_out, basis


def solution(mesh):
    return jax.shard_map(
        functools.partial(per_device, mesh.shape["narrow"], mesh.shape["wide"]),
        mesh=mesh,
        in_specs=(P(None, "narrow", "wide", None), P(), P(), P()),
        out_specs=(P("narrow", "wide", None, None), P()),
        check_vma=False,
    )
```

```python
import functools

import jax
import jax.numpy as jnp
from jax import lax
from jax.experimental import pallas as pl
from jax.experimental.pallas import tpu as pltpu
from jax.sharding import PartitionSpec as P

I2 = 256
I3 = 64
M = 128
SUB = 2

F32 = jnp.float32
BF16 = jnp.bfloat16
HIGH = lax.Precision.HIGHEST
NT = (((1,), (1,)), ((), ()))
TN = (((0,), (0,)), ((), ()))
MESH = pl.DeviceIdType.MESH


def split(x):
    hi = x.astype(BF16)
    return hi, (x - hi.astype(F32)).astype(BF16)


def gather_rows(ref, first, group):
    block = jnp.swapaxes(ref[:, pl.ds(pl.multiple_of(first, group), group), :], 0, 1)
    return jnp.concatenate([block[t] for t in range(group)], axis=1)


def gram_kernel(group, table_ref, gram_ref, acc, cross):
    rows = table_ref.shape[1]
    step = pl.program_id(0)

    @pl.when(step == 0)
    def _():
        acc[...] = jnp.zeros_like(acc)
        cross[...] = jnp.zeros_like(cross)

    def body(g, carry):
        hi, lo = split(gather_rows(table_ref, g * group, group))
        acc[...] += lax.dot_general(hi, hi, NT, preferred_element_type=F32)
        cross[...] += lax.dot_general(hi, lo, NT, preferred_element_type=F32)
        return carry

    lax.fori_loop(0, rows // group, body, 0)

    @pl.when(step == pl.num_programs(0) - 1)
    def _():
        gram_ref[...] = acc[...] + (cross[...] + cross[...].T)


def gram_of(flat):
    order, rows, cells = flat.shape
    block = min(32, rows)
    return pl.pallas_call(
        functools.partial(gram_kernel, block),
        grid=(rows // block,),
        in_specs=[pl.BlockSpec((order, block, cells), lambda i: (0, i, 0))],
        out_specs=pl.BlockSpec((order, order), lambda i: (0, 0)),
        out_shape=jax.ShapeDtypeStruct((order, order), F32),
        scratch_shapes=[pltpu.VMEM((order, order), F32)] * 2,
        compiler_params=pltpu.CompilerParams(vmem_limit_bytes=48 << 20),
    )(flat)


def greet(narrow, wide, at, place):
    barrier = pltpu.get_barrier_semaphore()
    for d in range(1, narrow):
        pl.semaphore_signal(
            barrier, inc=1, device_id={"narrow": lax.rem(at + d, narrow)}, device_id_type=MESH
        )
    for d in range(1, wide):
        pl.semaphore_signal(
            barrier, inc=1, device_id={"wide": lax.rem(place + d, wide)}, device_id_type=MESH
        )


def send(src, dst, send_sem, recv_sem, axis, to):
    copy = pltpu.make_async_remote_copy(
        src_ref=src,
        dst_ref=dst,
        send_sem=send_sem,
        recv_sem=recv_sem,
        device_id={axis: to},
        device_id_type=MESH,
    )
    copy.start()
    return copy


def finish(copies):
    for copy in copies:
        copy.wait()


def basis_kernel(
    narrow, wide, scale, part_ref, prior_ref, turned_ref,
    box_n, mine, box_w, full, square, sn, rn, sw, rw, tw, vw, tn, vn,
):
    at, place = lax.axis_index("narrow"), lax.axis_index("wide")
    greet(narrow, wide, at, place)
    pl.semaphore_wait(pltpu.get_barrier_semaphore(), narrow + wide - 2)
    copies = []
    for d in range(1, narrow):
        to = lax.rem(at + d, narrow)
        copies.append(send(part_ref.at[to], box_n.at[d], sn.at[d], rn.at[d], "narrow", to))
    finish(copies)
    value = part_ref[at]
    for d in range(1, narrow):
        value = value + box_n[d]
    mine[...] = value
    copies = []
    for d in range(1, wide):
        to = lax.rem(place + d, wide)
        copies.append(send(mine.at[to], box_w.at[d], sw.at[d], rw.at[d], "wide", to))
    finish(copies)
    value = mine[place]
    for d in range(1, wide):
        value = value + box_w[d]
    full[at, place] = value * scale
    copies = []
    for d in range(1, wide):
        to = lax.rem(place + d, wide)
        own = full.at[at, place]
        copies.append(send(own, own, tw.at[d], vw.at[d], "wide", to))
    finish(copies)
    copies = []
    for d in range(1, narrow):
        to = lax.rem(at + d, narrow)
        own = full.at[at]
        copies.append(send(own, own, tn.at[d], vn.at[d], "narrow", to))
    finish(copies)
    small = full.shape[2]
    for i in range(narrow * wide):
        square[i * small : (i + 1) * small, :] = full[i // wide, i % wide]
    gram = square[...]
    basis = prior_ref[...].T
    rank = basis.shape[1]
    row = lax.broadcasted_iota(jnp.int32, (rank, 1), 0)
    lane = lax.broadcasted_iota(jnp.int32, (rank, rank), 1)
    unit = jnp.where(lane == lax.broadcasted_iota(jnp.int32, (rank, rank), 0), 1.0, 0.0)
    for _ in range(SUB):
        q = jnp.dot(gram, basis, precision=HIGH, preferred_element_type=F32)
        s = lax.dot_general(q, q, TN, precision=HIGH, preferred_element_type=F32)
        pair = jnp.concatenate([s, unit], axis=1)
        root = jnp.ones((rank, 1), F32)
        for k in range(rank):
            line = pair[k : k + 1, :]
            pivot = line[:, k : k + 1]
            root = jnp.where(row == k, pivot, root)
            factor = jnp.where(row > k, pair[:, k : k + 1], 0.0)
            pair = pair - factor * (line / pivot)
        inverse = pair[:, rank:] * lax.rsqrt(root)
        basis = lax.dot_general(q, inverse, NT, precision=HIGH, preferred_element_type=F32)
    turned_ref[...] = basis.T


def basis_of(narrow, wide, gram, prior):
    scale = 1.0 / float(I2 * I3 * M)
    order, rank = prior.shape
    small = order // (narrow * wide)
    dma = pltpu.SemaphoreType.DMA
    return pl.pallas_call(
        functools.partial(basis_kernel, narrow, wide, scale),
        in_specs=[pl.BlockSpec(memory_space=pltpu.VMEM)] * 2,
        out_specs=pl.BlockSpec(memory_space=pltpu.VMEM),
        out_shape=jax.ShapeDtypeStruct((rank, order), F32),
        scratch_shapes=[
            pltpu.VMEM((narrow, wide, small, order), F32),
            pltpu.VMEM((wide, small, order), F32),
            pltpu.VMEM((wide, small, order), F32),
            pltpu.VMEM((narrow, wide, small, order), F32),
            pltpu.VMEM((order, order), F32),
            dma((narrow,)), dma((narrow,)),
            dma((wide,)), dma((wide,)),
            dma((wide,)), dma((wide,)),
            dma((narrow,)), dma((narrow,)),
        ],
        compiler_params=pltpu.CompilerParams(collective_id=1, has_side_effects=True),
    )(gram.reshape(narrow, wide, small, order), prior.T)


def project_kernel(
    group, depth, narrow, wide, spread, turned_ref, two_ref, table_ref, out_ref,
    trunc, second, core_box, chip_box, wide_box, sc, rc, sy, ry, sw, rw,
):
    _, rows, cells = table_ref.shape
    rank = turned_ref.shape[0]
    total = trunc.shape[0] // rank
    tall = total // depth
    step = pl.program_id(0)
    at, place = lax.axis_index("narrow"), lax.axis_index("wide")

    @pl.when(step == 0)
    def _():
        greet(narrow, wide, at, place)

    left_hi, left_lo = split(turned_ref[...])
    left = jnp.concatenate([left_hi, left_lo], axis=0)

    def body(g, carry):
        hi, lo = split(gather_rows(table_ref, g * group, group))
        both = jnp.dot(left, hi, preferred_element_type=F32)
        value = both[:rank] + (both[rank:] + jnp.dot(left_hi, lo, preferred_element_type=F32))
        for t in range(group):
            spot = step * rows + g * group + t
            spot = lax.rem(spot, depth) * tall + spot // depth
            trunc[pl.ds(spot, rank, stride=total), :] = value[:, t * cells : (t + 1) * cells]
        return carry

    lax.fori_loop(0, rows // group, body, 0)

    @pl.when(step == pl.num_programs(0) - 1)
    def _():
        pl.semaphore_wait(pltpu.get_barrier_semaphore(), narrow + wide - 2)
        two_hi, two_lo = split(two_ref[...])
        two = jnp.concatenate([two_hi, two_lo], axis=0)
        width = two_ref.shape[0]
        per = rank // narrow
        slab = width * depth
        chips = narrow // 2
        chip, core = at // 2, lax.rem(at, 2)
        chunk, chunks = 1, per
        flat = second.reshape(rank * slab, cells)

        def compute(block, q):
            def one(k, carry):
                r = block * per + q * chunk + k
                parts = [
                    trunc[pl.ds(pl.multiple_of(r * total + j * tall, tall), tall), :]
                    for j in range(depth)
                ]
                hi, lo = split(jnp.concatenate(parts, axis=1))
                both = jnp.dot(two, hi, preferred_element_type=F32)
                value = both[:width] + (
                    both[width:] + jnp.dot(two_hi, lo, preferred_element_type=F32)
                )
                for j in range(depth):
                    flat[pl.ds(r * slab + j, width, stride=depth), :] = value[
                        :, j * cells : (j + 1) * cells
                    ]
                return carry

            lax.fori_loop(0, chunk, one, 0)

        def part(q):
            return pl.ds(q * chunk, chunk)

        def target(h):
            return lax.rem(chip + h, chips)

        to_core, to_chip, to_wide = {}, {}, []

        def start(h, q):
            other = target(h) * 2 + (1 - core)
            compute(other, q)
            to_core[h, q] = send(
                second.at[other, part(q)], core_box.at[h, part(q)],
                sc.at[h, q], rc.at[h, q], "narrow", chip * 2 + (1 - core),
            )
            compute(target(h) * 2 + core, q)

        def merge(h, q):
            to_core[h, q].wait_recv()
            block = target(h) * 2 + core
            second[block, part(q)] = second[block, part(q)] + core_box[h, part(q)]
            if h:
                to_chip[h, q] = send(
                    second.at[block, part(q)], chip_box.at[h - 1, part(q)],
                    sy.at[h, q], ry.at[h, q], "narrow", block,
                )

        pairs = [(h, q) for h in [*range(1, chips), 0] for q in range(chunks)]
        for i, pair in enumerate(pairs):
            start(*pair)
            if i:
                merge(*pairs[i - 1])
        merge(*pairs[-1])
        for q in range(chunks):
            value = second[at, part(q)]
            for h in range(1, chips):
                to_chip[h, q].wait_recv()
                value = value + chip_box[h - 1, part(q)]
            if not spread:
                out_ref[0, part(q)] = value
                continue
            second[at, part(q)] = value
            band = slab // wide
            for d in range(1, wide):
                to = lax.rem(place + d, wide)
                rows_to = pl.ds(pl.multiple_of(to * band, band), band)
                to_wide.append(
                    send(
                        second.at[at, part(q), rows_to], wide_box.at[place, part(q)],
                        sw.at[d, q], rw.at[d, q], "wide", to,
                    )
                )
            own = pl.ds(pl.multiple_of(place * band, band), band)
            out_ref[place, part(q)] = second[at, part(q), own]
        for copy in [*to_core.values(), *to_chip.values()]:
            copy.wait_send()
        finish(to_wide)
        if spread:
            for d in range(1, wide):
                source = lax.rem(place + d, wide)
                out_ref[source] = wide_box[source]


def project(narrow, wide, turned, two, flat, depth):
    order, rows, cells = flat.shape
    rank, width = turned.shape[0], two.shape[0]
    block = min(32, rows)
    per, slab, chips = rank // narrow, width * depth, narrow // 2
    spread = (slab // wide) % 8 == 0
    shape = (wide, per, slab // wide, cells) if spread else (1, per, slab, cells)
    chunks = per
    dma = pltpu.SemaphoreType.DMA
    out = pl.pallas_call(
        functools.partial(
            project_kernel, min(16, block), depth, narrow, wide, spread
        ),
        grid=(rows // block,),
        in_specs=[
            pl.BlockSpec(turned.shape, lambda i: (0, 0)),
            pl.BlockSpec(two.shape, lambda i: (0, 0)),
            pl.BlockSpec((order, block, cells), lambda i: (0, i, 0)),
        ],
        out_specs=pl.BlockSpec(shape, lambda i: (0, 0, 0, 0)),
        out_shape=jax.ShapeDtypeStruct(shape, F32),
        scratch_shapes=[
            pltpu.VMEM((rank * rows, cells), F32),
            pltpu.VMEM((narrow, per, slab, cells), F32),
            pltpu.VMEM((chips, per, slab, cells), F32),
            pltpu.VMEM((max(chips - 1, 1), per, slab, cells), F32),
            pltpu.VMEM(shape, F32),
            dma((chips, chunks)), dma((chips, chunks)),
            dma((chips, chunks)), dma((chips, chunks)),
            dma((wide, chunks)), dma((wide, chunks)),
        ],
        compiler_params=pltpu.CompilerParams(
            vmem_limit_bytes=56 << 20, collective_id=2, has_side_effects=True
        ),
    )(turned, two, flat)
    if not spread:
        out = out.reshape(per, wide, slab // wide, cells)
        out = lax.all_to_all(out, "wide", split_axis=1, concat_axis=1, tiled=True)
        out = out.transpose(1, 0, 2, 3)
    return out.reshape(wide, per, width // wide, depth, cells)


def per_device(narrow, wide, table, prior_one, factor_two, factor_three):
    order, rows_two, rows_three, cells = table.shape
    flat = table.reshape(order, rows_two * rows_three, cells)
    turned = basis_of(narrow, wide, gram_of(flat), prior_one)
    at = lax.axis_index("narrow")
    two = lax.dynamic_slice_in_dim(factor_two, at * rows_two, rows_two, 0).T
    spread = project(narrow, wide, turned, two, flat, rows_three)
    three = factor_three.reshape(wide, rows_three, factor_three.shape[1])
    core_out = jnp.einsum("wrbjm,wjc->rbcm", spread, three, precision=HIGH)
    return core_out, turned.T


def solution(mesh):
    return jax.shard_map(
        functools.partial(per_device, mesh.shape["narrow"], mesh.shape["wide"]),
        mesh=mesh,
        in_specs=(P(None, "narrow", "wide", None), P(), P(), P()),
        out_specs=(P("narrow", "wide", None, None), P()),
        check_vma=False,
    )
```
